32 devices in a mesh: dp: 2 (over x), expert: 16 (over z, y, core).
Axes of the slice: x: 2, y: 2, z: 4, core: 2. Of those that a mesh axis runs over, the one named last changes fastest.
Arguments:
- tokens: bfloat16 [4096, 1792], P(('dp', 'expert')), may hold values from -6 to 6
- routes: int32 [4096, 4], P(('dp', 'expert')), may hold values from 0 to 15, all different within a row; in each aligned block of 128 rows (0 to 127, 128 to 255, ...) at most 64 rows name the same one
- route_weight: float32 [4096, 4], P(('dp', 'expert')), may hold values from 0.1 to 1
- w_in: float32 [16, 2, 1792, 1280], P('expert', None, 'dp'), may hold values from -0.125 to 0.125
- m_in: float32 [16, 2, 1792, 1280], P('expert', None, 'dp'), may hold values from -6 to 6
- v_in: float32 [16, 2, 1792, 1280], P('expert', None, 'dp'), may hold values from 0.5 to 20
- g_in: bfloat16 [16, 2, 1792, 1280], P('expert', None, 'dp'), may hold values from -30 to 30
- w_out: float32 [16, 1280, 1792], P('expert', 'dp'), may hold values from -0.15625 to 0.15625
- m_out: float32 [16, 1280, 1792], P('expert', 'dp'), may hold values from -6 to 6
- v_out: float32 [16, 1280, 1792], P('expert', 'dp'), may hold values from 0.5 to 20
- g_out: bfloat16 [16, 1280, 1792], P('expert', 'dp'), may hold values from -30 to 30
Outputs:
- mixed: bfloat16 [4096, 1792], P(('dp', 'expert'))
The draws below stay inside these ranges and needn't reach their ends.
Inputs may be any that keep to these rules, and one draw needn't show every extreme that they name: `routes`: A token's 4 experts differ. Within the rows of one device (aligned blocks of 128 tokens) each expert is named at most 64 times, a bound that some block reaches.
All inputs are finite; a program needn't handle non-finite values.
Results may differ from the reference program's by a relative error of at most 0.008.
Values may be sent and summed in bfloat16 or wider, within the bound.
No kernel may reach another device: no remote copies, remote signals or barrier semaphores. Data moves between devices by JAX's collectives and lax.ppermute only.
A program may use at most 128 MiB of HBM per device.

```python
import math
import jax
import jax.numpy as jnp
import numpy as np
from jax import lax

D = 1792
HIDDEN_SIZE = 1280
TOPW = 4
TOK_DEV = 128
EXPERTS = 16
CAP = 64
TOKENS = 4096
N_DP = 2
N_EXPERT = 16


def block_scale(key, extent, shards, smallest, high):
    loudness = 1.0
    for dim, blocks in shards:
        steps = jax.random.uniform(jax.random.fold_in(jax.random.fold_in(key, 6), dim), (blocks,), jnp.float32, smallest / len(shards), high / len(shards))
        loudness = loudness * jnp.repeat(jnp.exp(steps), extent[dim] // blocks).reshape((-1,) + (1,) * (len(extent) - 1 - dim))
    return loudness


def shared_out(rng, own, number, rows, number_of, top, reach, slope):
    sequence = jax.random.permutation(rng, number_of)
    packed, ordinary = shares(number_of, rows * top, reach, slope, True), shares(number_of, rows * top, reach, slope, False)
    places = jnp.arange(number_of)

    def named(tallies, rotation):
        used = int((tallies > 0).sum())
        fixed = max(1, used // 4)
        passed = fixed + (places - fixed + rotation * (used - fixed)) % max(1, number_of - fixed)
        return jnp.zeros((number_of,), jnp.int32).at[sequence[jnp.where(places < fixed, places, passed)]].set(jnp.asarray(tallies, jnp.int32))

    tallies = jnp.where(number % 4 == 0, named(packed, number // 4), named(ordinary, number - number // 4 - 1))
    mixed = jax.random.permutation(jax.random.fold_in(own, 3), number_of)
    giver, receiver = mixed[0:number_of // 2 * 2:2], mixed[1:number_of // 2 * 2:2]
    slack = jnp.minimum(tallies[giver] - 1, reach - tallies[receiver]) // 2
    slack = jnp.where((giver == sequence[0]) | (receiver == sequence[0]) | (tallies[receiver] == 0), 0, jnp.maximum(slack, 0))
    passed = jax.random.randint(jax.random.fold_in(own, 4), (number_of // 2,), 0, 1 << 20) % (slack + 1)
    tallies = tallies.at[giver].add(-passed).at[receiver].add(passed)
    members = jnp.searchsorted(jnp.cumsum(tallies), jnp.arange(rows * top), side="right").astype(jnp.int32)
    grid = members.reshape(top, rows).T
    grid = grid[jax.random.permutation(jax.random.fold_in(own, 1), rows)]
    rotation = jax.random.randint(jax.random.fold_in(own, 2), (rows, 1), 0, top)
    return jnp.take_along_axis(grid, (jnp.arange(top)[None, :] + rotation) % top, axis=1)


def shares(count, total, most, slope, full):
    loads = [(1 << 20) // math.isqrt(rank ** slope) + 1 for rank in range(1, count + 1)]
    largest = most if full else min(most, max(-(-total // count), total * loads[0] // sum(loads)))
    least = 1 if total - largest >= count - 1 else 0
    counts, rest = [largest] + [least] * (count - 1), total - largest - least * (count - 1)
    while rest > 0:
        free = [i for i in range(1, count) if counts[i] < largest] or [i for i in range(1, count) if counts[i] < most]
        pool, budget = sum([loads[i] for i in free]), rest
        for i in free:
            more = min(most - counts[i], max(1, budget * loads[i] // pool), rest)
            counts[i] = counts[i] + more
            rest = rest - more
    return np.array(counts)


def gaussian(own_key, shape, spread, reach, cuts=(), kind=jnp.bfloat16):
    gain = block_scale(own_key, shape, cuts, -0.22, 0.18) if cuts else 1.0
    values = jax.random.normal(own_key, shape, jnp.float32) * spread * gain
    return jnp.minimum(jnp.maximum(values, -reach), reach).astype(kind)


def setup_inputs(seed: int = 0) -> dict:
    arg_keys = jax.random.split(jax.random.key(seed), 12)
    tokens = gaussian(arg_keys[0], (TOKENS, D), 1.0, 6.0, ((0, 32),))
    routes_keys = jax.random.split(jax.random.fold_in(arg_keys[1], 1), TOKENS // TOK_DEV)
    routes_turns = jax.random.permutation(jax.random.fold_in(arg_keys[1], 3), TOKENS // TOK_DEV)
    routes = jax.vmap(lambda own, number: shared_out(jax.random.fold_in(arg_keys[1], 2), own, number, TOK_DEV, EXPERTS, TOPW, CAP, 2))(routes_keys, routes_turns).reshape((TOKENS, TOPW))
    route_weight = jnp.clip(0.1 + 0.9 * jax.random.uniform(arg_keys[2], (TOKENS, TOPW), jnp.float32) ** block_scale(arg_keys[2], (TOKENS, TOPW), ((0, 32),), -0.2, 0.2), 0.1, 1.0)
    w_in = gaussian(arg_keys[3], (EXPERTS, 2, D, HIDDEN_SIZE), D ** -0.5, 0.125, ((0, 16), (2, 2)), jnp.float32)
    m_in = gaussian(arg_keys[4], (EXPERTS, 2, D, HIDDEN_SIZE), 1.0, 6.0, ((0, 16), (2, 2)), jnp.float32)
    v_in = jnp.clip(jnp.exp(math.log(20.0) - 3.6888795 * jax.random.uniform(arg_keys[5], (EXPERTS, 2, D, HIDDEN_SIZE), jnp.float32) ** block_scale(arg_keys[5], (EXPERTS, 2, D, HIDDEN_SIZE), ((0, 16), (2, 2)), -0.2, 0.2)), 0.5, 20.0)
    g_in = gaussian(arg_keys[6], (EXPERTS, 2, D, HIDDEN_SIZE), 5.0, 30.0, ((0, 16), (2, 2)))
    w_out = gaussian(arg_keys[7], (EXPERTS, HIDDEN_SIZE, D), HIDDEN_SIZE ** -0.5, 0.15625, ((0, 16), (1, 2)), jnp.float32)
    m_out = gaussian(arg_keys[8], (EXPERTS, HIDDEN_SIZE, D), 1.0, 6.0, ((0, 16), (1, 2)), jnp.float32)
    v_out = jnp.clip(jnp.exp(math.log(20.0) - 3.6888795 * jax.random.uniform(arg_keys[9], (EXPERTS, HIDDEN_SIZE, D), jnp.float32) ** block_scale(arg_keys[9], (EXPERTS, HIDDEN_SIZE, D), ((0, 16), (1, 2)), -0.2, 0.2)), 0.5, 20.0)
    g_out = gaussian(arg_keys[10], (EXPERTS, HIDDEN_SIZE, D), 5.0, 30.0, ((0, 16), (1, 2)))
    return dict(tokens=tokens, routes=routes, route_weight=route_weight, w_in=w_in, m_in=m_in, v_in=v_in, g_in=g_in, w_out=w_out, m_out=m_out, v_out=v_out, g_out=g_out)


beta_one = 0.9
beta_two = 0.95
corr_one = 0.99997343860111
corr_two = 0.99407947077967
adam_eps = 1e-08
learn_rate = 0.01
weight_decay = 0.1

def adamw(master, moment, second, gradient):
    grad_value = gradient.astype(jnp.float32)
    moment_new = beta_one * moment + (1.0 - beta_one) * grad_value
    second_new = beta_two * second + (1.0 - beta_two) * grad_value * grad_value
    update = moment_new / corr_one / (jnp.sqrt(second_new / corr_two) + adam_eps)
    return (master - learn_rate * (update + weight_decay * master)).astype(jnp.bfloat16)

def reference(tokens, routes, route_weight, w_in, m_in, v_in, g_in, w_out, m_out, v_out, g_out):
    limit = N_DP * N_EXPERT * CAP
    entry_count = TOKENS * TOPW
    flat_routes = routes.reshape(-1)
    owners = jnp.arange(entry_count, dtype=jnp.int32) // TOPW
    flat_weight = route_weight.reshape(-1)
    positions = jnp.arange(limit, dtype=jnp.int32)

    def one_expert(totals, inputs):
        expert_id, master_in, moment_in, second_in, grad_in, master_out, moment_out, second_out, grad_out = inputs
        gate_up = adamw(master_in, moment_in, second_in, grad_in)
        down_proj = adamw(master_out, moment_out, second_out, grad_out)
        hits = flat_routes == expert_id
        picks = jnp.nonzero(hits, size=limit, fill_value=0)[0].astype(jnp.int32)
        valid = (positions < jnp.sum(hits.astype(jnp.int32))).astype(jnp.float32)
        token_ids = jnp.take(owners, picks).astype(jnp.int32)
        block_rows = jnp.take(tokens, token_ids, axis=0)
        gate_pre = jnp.dot(block_rows, gate_up[0], preferred_element_type=jnp.float32)
        up_pre = jnp.dot(block_rows, gate_up[1], preferred_element_type=jnp.float32)
        hidden = (jax.nn.silu(gate_pre) * up_pre).astype(jnp.bfloat16)
        results = jnp.dot(hidden, down_proj, preferred_element_type=jnp.float32).astype(jnp.bfloat16)
        scaled = results.astype(jnp.float32) * (jnp.take(flat_weight, picks) * valid)[:, None]
        return (totals.at[token_ids].add(scaled), None)
    scanned = lax.scan(one_expert, jnp.zeros((TOKENS, D), jnp.float32), (jnp.arange(EXPERTS, dtype=jnp.int32), w_in, m_in, v_in, g_in, w_out, m_out, v_out, g_out))
    return scanned[0].astype(jnp.bfloat16)
```

```python
import functools

import jax
import jax.numpy as jnp
from jax import lax
from jax.experimental import pallas as pl
from jax.experimental.pallas import tpu as pltpu
from jax.sharding import Mesh, PartitionSpec as P


beta_one = 0.9
beta_two = 0.95
corr_one = 0.99997343860111
corr_two = 0.99407947077967
adam_eps = 1e-08
learn_rate = 0.01
weight_decay = 0.1

LANES = 128
PAIR = 2


def adamw(master, moment, second, gradient):
    grad_value = gradient.astype(jnp.float32)
    moment_new = beta_one * moment + (1.0 - beta_one) * grad_value
    second_new = beta_two * second + (1.0 - beta_two) * grad_value * grad_value
    update = moment_new / corr_one / (jnp.sqrt(second_new / corr_two) + adam_eps)
    return (master - learn_rate * (update + weight_decay * master)).astype(jnp.bfloat16)


def ring(size):
    return [(i, (i + 1) % size) for i in range(size)]


def shift(value, axis):
    return lax.ppermute(value, axis, ring(lax.axis_size(axis)))


def add(one, two):
    return (one.astype(jnp.float32) + two.astype(jnp.float32)).astype(jnp.bfloat16)


def expert_kernel(sizes, *refs):
    blocks, peers, parts, capacity, head = sizes
    offsets, info = refs[0], refs[1]
    token_refs = refs[2 : 2 + blocks]
    refs = refs[2 + blocks :]
    proj_hbm = [refs[i * parts : (i + 1) * parts] for i in range(2)]
    refs = refs[2 * parts :]
    down_hbm = refs[:2]
    refs = refs[2:]
    far_out = refs[0]
    near_outs = refs[1 : 1 + peers]
    tail_outs = refs[1 + peers : 1 + 2 * peers]
    refs = refs[1 + 2 * peers :]
    proj_vmem, down_vmem, rows_buf, hidden_buf, out_buf, sems = refs
    tokens, width = token_refs[0].shape
    depth = width // parts
    rows = blocks * capacity

    copies = []
    for e in range(2):
        for p in range(parts):
            copies.append(
                pltpu.make_async_copy(proj_hbm[e][p], proj_vmem.at[e, p], sems.at[e * (parts + 1) + p])
            )
        copies.append(
            pltpu.make_async_copy(down_hbm[e], down_vmem.at[e], sems.at[e * (parts + 1) + parts])
        )
    for copy in copies:
        copy.start()

    slots = lax.broadcasted_iota(jnp.int32, (capacity, tokens), 0).astype(jnp.float32)

    def picks(b):
        return [(slots == info[4 * b + e : 4 * b + e + 1, :]) for e in range(2)]

    for b in range(blocks):
        chosen = jnp.concatenate(picks(b), axis=0).astype(jnp.bfloat16)
        for p in range(parts):
            if parts == 1:
                block = token_refs[b][...]
            else:
                start = pl.multiple_of(offsets[p] * LANES, LANES)
                block = token_refs[b][:, pl.ds(start, depth)]
            got = jnp.dot(chosen, block, preferred_element_type=jnp.float32).astype(jnp.bfloat16)
            for e in range(2):
                rows_buf[e, p, b * capacity : (b + 1) * capacity, :] = got[
                    e * capacity : (e + 1) * capacity
                ]

    for e in range(2):
        for p in range(parts):
            copies[e * (parts + 1) + p].wait()
        sums = [None, None]
        for side in range(2):
            for p in range(parts):
                term = jnp.dot(
                    rows_buf[e, p], proj_vmem[e, p, side], preferred_element_type=jnp.float32
                )
                sums[side] = term if sums[side] is None else sums[side] + term
        gate, up = sums
        hidden_buf[...] = (gate / (1.0 + jnp.exp(-gate)) * up).astype(jnp.bfloat16)
        copies[e * (parts + 1) + parts].wait()
        result = jnp.dot(hidden_buf[...], down_vmem[e], preferred_element_type=jnp.float32)
        for b in range(blocks):
            weight = info[4 * b + 2 + e : 4 * b + 3 + e, :]
            scale = jnp.sum(jnp.where(picks(b)[e], weight, 0.0), axis=1, keepdims=True)
            out_buf[b, e * capacity : (e + 1) * capacity, :] = (
                result[b * capacity : (b + 1) * capacity] * scale
            ).astype(jnp.bfloat16)

    for b in range(blocks):
        chosen = jnp.concatenate(picks(b), axis=0).astype(jnp.bfloat16)
        total = lax.dot_general(
            chosen, out_buf[b], (((0,), (0,)), ((), ())), preferred_element_type=jnp.float32
        ).astype(jnp.bfloat16)
        peer, far = b // 2, b % 2
        tail_outs[peer][far * tokens : (far + 1) * tokens, :] = total[:, head:]
        if far:
            far_out[peer * tokens : (peer + 1) * tokens, :] = total[:, :head]
        else:
            near_outs[peer][...] = total[:, :head]


def expert_group(offsets, info, blocks, projs, downs, capacity, head):
    count = len(blocks)
    peers = count // 2
    tokens, width = blocks[0].shape
    parts = len(projs[0])
    half = downs[0].shape[0]
    depth = width // parts
    rows = count * capacity
    tail = width - head
    outs = [jax.ShapeDtypeStruct((peers * tokens, head), jnp.bfloat16)]
    outs += [jax.ShapeDtypeStruct((tokens, head), jnp.bfloat16)] * peers
    outs += [jax.ShapeDtypeStruct((2 * tokens, tail), jnp.bfloat16)] * peers
    vmem = pl.BlockSpec(memory_space=pltpu.VMEM)
    flops = 2 * 2 * rows * width * half * 3
    result = pl.pallas_call(
        functools.partial(expert_kernel, (count, peers, parts, capacity, head)),
        out_shape=outs,
        in_specs=[pl.BlockSpec(memory_space=pltpu.SMEM), vmem]
        + [vmem] * count
        + [pl.BlockSpec(memory_space=pl.ANY)] * (2 * parts + 2),
        out_specs=[vmem] * len(outs),
        scratch_shapes=[
            pltpu.VMEM((2, parts, 2, depth, half), jnp.bfloat16),
            pltpu.VMEM((2, half, width), jnp.bfloat16),
            pltpu.VMEM((2, parts, rows, depth), jnp.bfloat16),
            pltpu.VMEM((rows, half), jnp.bfloat16),
            pltpu.VMEM((count, 2 * capacity, width), jnp.bfloat16),
            pltpu.SemaphoreType.DMA((2 * (parts + 1),)),
        ],
        compiler_params=pltpu.CompilerParams(vmem_limit_bytes=48 << 20),
        cost_estimate=pl.CostEstimate(
            flops=flops, bytes_accessed=6 * width * half * 2 + 8 * tokens * width * count, transcendentals=2 * rows * half
        ),
        name="expert_group",
    )(offsets, info, *blocks, *projs[0], *projs[1], *downs)
    return result[0], result[1 : 1 + peers], result[1 + peers :]


def chain(own_first, axis):
    size = lax.axis_size(axis)
    if size == 1:
        return own_first[0]
    moving = shift(own_first[1], axis)
    for j in range(2, size):
        moving = shift(add(moving, own_first[j]), axis)
    return add(moving, own_first[0])


def per_device(tokens, routes, route_weight, w_in, m_in, v_in, g_in, w_out, m_out, v_out, g_out):
    deep, nz, ny = lax.axis_size("dpo"), lax.axis_size("z"), lax.axis_size("y")
    tok_rows, width = tokens.shape
    top_count = routes.shape[1]
    experts = nz * ny * 2
    capacity = 2 * tok_rows * top_count // experts
    xi, zi, yi, ci = (lax.axis_index(a) for a in ("x", "z", "y", "core"))
    swap = ring(2)
    everyone = ("dpo", "x", "z", "y", "core")

    far_tokens = lax.ppermute(tokens, "x", swap)
    held = [[tokens], [far_tokens]]
    for lane in held:
        for _ in range(nz - 1):
            lane.append(shift(lane[-1], "z"))
    grid_tokens = [[[held[f][g]] for f in range(2)] for g in range(nz)]
    for g in range(nz):
        for f in range(2):
            for _ in range(ny - 1):
                grid_tokens[g][f].append(shift(grid_tokens[g][f][-1], "y"))

    meta = jnp.concatenate([routes.T.astype(jnp.float32), route_weight.T], axis=0)
    total = deep * 2 * nz * ny * 2
    meta_all = lax.all_to_all(
        jnp.broadcast_to(meta[None], (total,) + meta.shape), everyone, split_axis=0, concat_axis=0, tiled=True
    )
    back_z = (zi - jnp.arange(nz)) % nz
    back_y = (yi - jnp.arange(ny)) % ny
    side = jnp.where(jnp.arange(2) == 0, xi, 1 - xi)
    places = (lax.axis_index("dpo") * 2 + side)[None, None, :]
    places = (places * nz + back_z[:, None, None]) * ny + back_y[None, :, None]
    places = places * 2 + ci
    meta_own = jnp.take(meta_all, places.reshape(-1), axis=0)
    names = meta_own[:, None, :top_count, :]
    route_scale = meta_own[:, None, top_count:, :]
    base = (zi * ny + yi) * 2
    wanted = jnp.stack([base + ci, base + 1 - ci]).astype(jnp.float32)
    same = names == wanted[None, :, None, None]
    hit = jnp.any(same, axis=2)
    weight = jnp.sum(jnp.where(same, route_scale, 0.0), axis=2)
    upto = (jnp.arange(tok_rows)[:, None] <= jnp.arange(tok_rows)[None, :]).astype(jnp.bfloat16)
    seen = jnp.dot(hit.astype(jnp.bfloat16).reshape(-1, tok_rows), upto, preferred_element_type=jnp.float32)
    rank = jnp.where(hit, seen.reshape(hit.shape) - 1.0, -1.0)
    info = jnp.concatenate([rank, weight], axis=1).reshape(nz, ny * 2 * 4, tok_rows)

    piece = w_in.shape[3] // (deep * 2)

    def half_of(parity):
        def cut(array):
            found = [
                lax.dynamic_slice_in_dim(array[0], (2 * j + parity) * piece, piece, axis=2)
                for j in range(deep)
            ]
            return found[0] if deep == 1 else jnp.concatenate(found, axis=2)

        return adamw(cut(w_in), cut(m_in), cut(v_in), cut(g_in))

    proj_sent = half_of(1 - xi)
    proj_far = lax.ppermute(proj_sent, "x", swap)
    proj_near = half_of(xi)
    down = adamw(w_out, m_out, v_out, g_out)[0]
    if deep == 1:
        proj = [proj_near, proj_far]
        offsets = jnp.stack([xi, 1 - xi]) * (width // 2 // LANES)
    else:
        both = jnp.where(xi == 0, jnp.stack([proj_near, proj_far], 1), jnp.stack([proj_far, proj_near], 1))
        full = lax.all_gather(both, "dpo", axis=1, tiled=True)
        proj = [full.reshape(2, width, -1)]
        offsets = jnp.zeros((1,), jnp.int32)
        down = lax.all_gather(down, "dpo", axis=0, tiled=True)
    other_proj = [lax.ppermute(p, "core", swap) for p in proj]
    other_down = lax.ppermute(down, "core", swap)

    head = (width // LANES * 9 // 14) * LANES
    summed = [None] * nz
    for g in list(range(1, nz)) + [0]:
        blocks = [grid_tokens[g][f][j] for j in range(ny) for f in range(2)]
        far_head, near_heads, tails = expert_group(
            offsets, info[g], blocks, [proj, other_proj], [down, other_down], capacity, head
        )
        back = lax.ppermute(far_head, "x", swap)
        heads = [
            add(near_heads[j], back[j * tok_rows : (j + 1) * tok_rows]) for j in range(ny)
        ]
        summed[g] = (chain(heads, "y"), chain(tails, "y"))
    head_done = chain([s[0] for s in summed], "z")
    tail_done = chain([s[1] for s in summed], "z")
    tail_back = lax.ppermute(tail_done[tok_rows:], "x", swap)
    return jnp.concatenate([head_done, add(tail_done[:tok_rows], tail_back)], axis=1)


def solution(mesh):
    deep = mesh.shape["dp"] // PAIR
    chips = mesh.shape["expert"] // 2
    ny = 1
    while ny * ny * 4 <= chips:
        ny *= 2
    nz = chips // ny
    fine = Mesh(mesh.devices.reshape(deep, PAIR, nz, ny, 2), ("dpo", "x", "z", "y", "core"))
    dp, expert = ("dpo", "x"), ("z", "y", "core")
    everyone = dp + expert
    placed = (
        P(everyone, None),
        P(everyone, None),
        P(everyone, None),
        P(expert, None, dp, None),
        P(expert, None, dp, None),
        P(expert, None, dp, None),
        P(expert, None, dp, None),
        P(expert, dp, None),
        P(expert, dp, None),
        P(expert, dp, None),
        P(expert, dp, None),
    )
    return jax.shard_map(
        per_device, mesh=fine, in_specs=placed, out_specs=P(everyone, None), check_vma=False
    )
```

```python
import functools

import jax
import jax.numpy as jnp
from jax import lax
from jax.experimental import pallas as pl
from jax.experimental.pallas import tpu as pltpu
from jax.sharding import Mesh, PartitionSpec as P


beta_one = 0.9
beta_two = 0.95
corr_one = 0.99997343860111
corr_two = 0.99407947077967
adam_eps = 1e-08
learn_rate = 0.01
weight_decay = 0.1

LANES = 128
PAIR = 2


def adamw(master, moment, second, gradient):
    grad_value = gradient.astype(jnp.float32)
    moment_new = beta_one * moment + (1.0 - beta_one) * grad_value
    second_new = beta_two * second + (1.0 - beta_two) * grad_value * grad_value
    update = moment_new / corr_one / (jnp.sqrt(second_new / corr_two) + adam_eps)
    return (master - learn_rate * (update + weight_decay * master)).astype(jnp.bfloat16)


def ring(size, by=1):
    return [(i, (i + by) % size) for i in range(size)]


def shift(value, axis, by=1):
    return lax.ppermute(value, axis, ring(lax.axis_size(axis), by))


def add(one, two):
    return (one.astype(jnp.float32) + two.astype(jnp.float32)).astype(jnp.bfloat16)


def load_weights(sources, targets, sems, first):
    return [
        pltpu.make_async_copy(source, target, sems.at[first + n])
        for n, (source, target) in enumerate(zip(sources, targets))
    ]


def picks(info, b, e, capacity):
    slots = lax.broadcasted_iota(jnp.int32, (capacity, info.shape[1]), 0).astype(jnp.float32)
    return slots == info[4 * b + e : 4 * b + e + 1, :]


def chosen(info, b, capacity):
    both = [picks(info, b, e, capacity) for e in range(2)]
    return jnp.concatenate(both, axis=0).astype(jnp.bfloat16)


def gather_rows(offsets, info, token_refs, rows_buf, parts, capacity):
    depth = token_refs[0].shape[1] // parts
    for b, token_ref in enumerate(token_refs):
        mine = chosen(info, b, capacity)
        for p in range(parts):
            if parts == 1:
                block = token_ref[...]
            else:
                start = pl.multiple_of(offsets[p] * LANES, LANES)
                block = token_ref[:, pl.ds(start, depth)]
            got = jnp.dot(mine, block, preferred_element_type=jnp.float32).astype(jnp.bfloat16)
            for e in range(2):
                rows_buf[e, p, b * capacity : (b + 1) * capacity, :] = got[
                    e * capacity : (e + 1) * capacity
                ]


def prepare_kernel(sizes, *refs):
    blocks, parts, capacity = sizes
    offsets, info = refs[0], refs[1]
    token_refs = refs[2 : 2 + blocks]
    refs = refs[2 + blocks :]
    near_hbm, down_hbm = refs[:2], refs[2:4]
    refs = refs[4:]
    if parts > 1:
        far_hbm, refs = refs[:2], refs[2:]
        near_vmem, down_vmem, rows_buf, sums_buf, far_vmem, sems = refs
        far = load_weights(far_hbm, [far_vmem.at[e] for e in range(2)], sems, 6)
    else:
        near_vmem, down_vmem, rows_buf, sums_buf, sems = refs
        far = []
    near = load_weights(
        [near_hbm[e].at[side] for e in range(2) for side in range(2)],
        [near_vmem.at[e, side] for e in range(2) for side in range(2)],
        sems,
        0,
    )
    down = load_weights(down_hbm, [down_vmem.at[e] for e in range(2)], sems, 4)
    for copy in near + far + down:
        copy.start()
    gather_rows(offsets, info, token_refs, rows_buf, parts, capacity)
    for e in range(2):
        for side in range(2):
            near[2 * e + side].wait()
            sums_buf[e, side] = jnp.dot(
                rows_buf[e, 0], near_vmem[e, side], preferred_element_type=jnp.float32
            )
    for e, copy in enumerate(far):
        copy.wait()
        sums_buf[e, 0] = sums_buf[e, 0] + jnp.dot(
            rows_buf[e, 1], far_vmem[e], preferred_element_type=jnp.float32
        )
    for copy in down:
        copy.wait()


def expert_kernel(sizes, *refs):
    blocks, peers, parts, capacity, head, load, ready = sizes
    offsets, info = refs[0], refs[1]
    refs = refs[2:]
    if ready:
        rows_buf, sums_buf = refs[:2]
        refs = refs[2:]
    else:
        token_refs = refs[:blocks]
        refs = refs[blocks:]
    near_vmem, down_vmem = refs[:2]
    refs = refs[2:]
    if parts > 1:
        gate_vmem = refs[0]
        refs = refs[1:]
        if load:
            far_hbm = refs[:2]
            refs = refs[2:]
        else:
            up_vmem = refs[0]
            refs = refs[1:]
    far_out = refs[0]
    near_outs = refs[1 : 1 + peers]
    tail_outs = refs[1 + peers : 1 + 2 * peers]
    refs = refs[1 + 2 * peers :]
    if parts > 1 and load:
        up_vmem, sems = refs[0], refs[-1]
        refs = refs[1:-1]
    hidden_buf, out_buf = refs[:2]
    if not ready:
        rows_buf = refs[2]

    copies = []
    if parts > 1 and load:
        copies = load_weights(far_hbm, [up_vmem.at[e] for e in range(2)], sems, 0)
        for copy in copies:
            copy.start()
    if not ready:
        gather_rows(offsets, info, token_refs, rows_buf, parts, capacity)

    for e in range(2):
        sums = []
        for side in range(2):
            if ready:
                value = sums_buf[e, side]
            else:
                value = jnp.dot(
                    rows_buf[e, 0], near_vmem[e, side], preferred_element_type=jnp.float32
                )
            if parts > 1 and not (ready and side == 0):
                if copies and side == 1:
                    copies[e].wait()
                weights = (gate_vmem, up_vmem)[side]
                value = value + jnp.dot(
                    rows_buf[e, 1], weights[e], preferred_element_type=jnp.float32
                )
            sums.append(value)
        gate, up = sums
        hidden_buf[...] = (gate / (1.0 + jnp.exp(-gate)) * up).astype(jnp.bfloat16)
        result = jnp.dot(hidden_buf[...], down_vmem[e], preferred_element_type=jnp.float32)
        for b in range(blocks):
            weight = info[4 * b + 2 + e : 4 * b + 3 + e, :]
            scale = jnp.sum(jnp.where(picks(info, b, e, capacity), weight, 0.0), axis=1, keepdims=True)
            out_buf[b, e * capacity : (e + 1) * capacity, :] = (
                result[b * capacity : (b + 1) * capacity] * scale
            ).astype(jnp.bfloat16)

    tokens = info.shape[1]
    for b in range(blocks):
        total = lax.dot_general(
            chosen(info, b, capacity),
            out_buf[b],
            (((0,), (0,)), ((), ())),
            preferred_element_type=jnp.float32,
        ).astype(jnp.bfloat16)
        peer, far = b // 2, b % 2
        tail_outs[peer][far * tokens : (far + 1) * tokens, :] = total[:, head:]
        if far:
            far_out[peer * tokens : (peer + 1) * tokens, :] = total[:, :head]
        else:
            near_outs[peer][...] = total[:, :head]


VMEM_SPEC = pl.BlockSpec(memory_space=pltpu.VMEM)
SMEM_SPEC = pl.BlockSpec(memory_space=pltpu.SMEM)
ANY_SPEC = pl.BlockSpec(memory_space=pl.ANY)


def prepare_group(offsets, info, blocks, nears, downs, fars, capacity):
    count = len(blocks)
    tokens, width = blocks[0].shape
    parts = offsets.shape[0]
    half = downs[0].shape[0]
    depth = width // parts
    rows = count * capacity
    outs = [
        pltpu.VMEM((2, 2, depth, half), jnp.bfloat16),
        pltpu.VMEM((2, half, width), jnp.bfloat16),
        pltpu.VMEM((2, parts, rows, depth), jnp.bfloat16),
        pltpu.VMEM((2, 2, rows, half), jnp.float32),
    ]
    operands = [*nears, *downs]
    if parts > 1:
        operands += fars
        outs.append(pltpu.VMEM((2, depth, half), jnp.bfloat16))
    result = pl.pallas_call(
        functools.partial(prepare_kernel, (count, parts, capacity)),
        out_shape=outs,
        in_specs=[SMEM_SPEC] + [VMEM_SPEC] * (1 + count) + [ANY_SPEC] * len(operands),
        out_specs=[VMEM_SPEC] * len(outs),
        scratch_shapes=[pltpu.SemaphoreType.DMA((8,))],
        compiler_params=pltpu.CompilerParams(vmem_limit_bytes=24 << 20),
        cost_estimate=pl.CostEstimate(
            flops=2 * 2 * rows * width * half,
            bytes_accessed=8 * width * half + 2 * tokens * width * count,
            transcendentals=0,
        ),
        name="prepare_group",
    )(offsets, info, *blocks, *operands)
    return result if parts > 1 else (*result, None)


def expert_group(
    offsets, info, blocks, prepared, near, down, far_gate, far_up, load, capacity, head
):
    parts = offsets.shape[0]
    half, width = down.shape[1:]
    tokens = info.shape[1]
    count = info.shape[0] // 4
    peers = count // 2
    rows = count * capacity
    depth = width // parts
    tail = width - head
    ready = prepared is not None
    inputs = list(prepared) if ready else list(blocks)
    operands = [*inputs, near, down]
    in_specs = [SMEM_SPEC] + [VMEM_SPEC] * (1 + len(operands))
    if parts > 1:
        operands += [far_gate, *far_up] if load else [far_gate, far_up]
        in_specs += [VMEM_SPEC] + ([ANY_SPEC] * 2 if load else [VMEM_SPEC])
    outs = [jax.ShapeDtypeStruct((peers * tokens, head), jnp.bfloat16)]
    outs += [jax.ShapeDtypeStruct((tokens, head), jnp.bfloat16)] * peers
    outs += [jax.ShapeDtypeStruct((2 * tokens, tail), jnp.bfloat16)] * peers
    scratch = [
        pltpu.VMEM((rows, half), jnp.bfloat16),
        pltpu.VMEM((count, 2 * capacity, width), jnp.bfloat16),
    ]
    if not ready:
        scratch.append(pltpu.VMEM((2, parts, rows, depth), jnp.bfloat16))
    if parts > 1 and load:
        outs.append(pltpu.VMEM((2, depth, half), jnp.bfloat16))
        scratch.append(pltpu.SemaphoreType.DMA((2,)))
    result = pl.pallas_call(
        functools.partial(expert_kernel, (count, peers, parts, capacity, head, load, ready)),
        out_shape=outs,
        in_specs=in_specs,
        out_specs=[VMEM_SPEC] * len(outs),
        scratch_shapes=scratch,
        compiler_params=pltpu.CompilerParams(vmem_limit_bytes=24 << 20),
        cost_estimate=pl.CostEstimate(
            flops=2 * 2 * rows * width * half * 3,
            bytes_accessed=8 * tokens * width * count,
            transcendentals=2 * rows * half,
        ),
        name="expert_group",
    )(offsets, info, *operands)
    if parts > 1 and load:
        far_up = result[-1]
    return result[0], result[1 : 1 + peers], result[1 + peers : 1 + 2 * peers], far_up


def chain(own_first, axis):
    size = lax.axis_size(axis)
    if size == 1:
        return own_first[0]
    moving = shift(own_first[1], axis)
    for j in range(2, size):
        moving = add(moving, own_first[j])
        moving = shift(moving, axis)
    return add(moving, own_first[0])


def layer(tokens, routes, route_weight, w_in, m_in, v_in, g_in, w_out, m_out, v_out, g_out):
    deep, nz, ny = lax.axis_size("dpo"), lax.axis_size("z"), lax.axis_size("y")
    tok_rows, width = tokens.shape
    top_count = routes.shape[1]
    experts = nz * ny * 2
    capacity = 2 * tok_rows * top_count // experts
    xi, zi, yi, ci = (lax.axis_index(a) for a in ("x", "z", "y", "core"))

    far_tokens = shift(tokens, "x")
    held = [[tokens], [far_tokens]]
    for f in range(2):
        for _ in range(1, nz):
            held[f].append(shift(held[f][-1], "z"))
    grid_tokens = [[[held[f][g]] for f in range(2)] for g in range(nz)]
    for g in range(nz):
        for f in range(2):
            for _ in range(1, ny):
                grid_tokens[g][f].append(shift(grid_tokens[g][f][-1], "y"))

    meta = jnp.concatenate([routes.T.astype(jnp.float32), route_weight.T], axis=0)
    meta = jnp.stack([meta, shift(meta, "x")])
    meta = jnp.stack([meta] + [shift(meta, "z", j) for j in range(1, nz)])
    meta = jnp.stack([meta] + [shift(meta, "y", j) for j in range(1, ny)], axis=1)
    meta_own = meta.reshape((-1,) + meta.shape[3:])
    names = meta_own[:, None, :top_count, :]
    route_scale = meta_own[:, None, top_count:, :]
    base = (zi * ny + yi) * 2
    wanted = jnp.stack([base + ci, base + 1 - ci]).astype(jnp.float32)
    same = names == wanted[None, :, None, None]
    hit = jnp.any(same, axis=2)
    weight = jnp.sum(jnp.where(same, route_scale, 0.0), axis=2)
    upto = (jnp.arange(tok_rows)[:, None] <= jnp.arange(tok_rows)[None, :]).astype(jnp.bfloat16)
    seen = jnp.dot(hit.astype(jnp.bfloat16).reshape(-1, tok_rows), upto, preferred_element_type=jnp.float32)
    rank = jnp.where(hit, seen.reshape(hit.shape) - 1.0, -1.0)
    info = jnp.concatenate([rank, weight], axis=1).reshape(nz, ny * 2 * 4, tok_rows)

    piece = w_in.shape[3] // (deep * 2)

    def half_of(parity, arrays, first, count):
        def cut(array):
            rows = array.shape[2]
            found = [
                lax.dynamic_slice(
                    array, (0, first, 0, (2 * j + parity) * piece), (1, count, rows, piece)
                )
                for j in range(deep)
            ]
            return found[0] if deep == 1 else jnp.concatenate(found, axis=-1)

        return adamw(*[cut(a) for a in arrays])[0]

    state = (w_in, m_in, v_in, g_in)
    proj_far, sent = [], None
    for side in range(2):
        if sent is not None:
            *state, sent = lax.optimization_barrier((*state, sent))
        sent = half_of(1 - xi, state, side, 1)[0]
        proj_far.append(shift(sent, "x"))
    *state, sent = lax.optimization_barrier((*state, sent))
    proj_near = half_of(xi, state, 0, 2)
    down = adamw(w_out, m_out, v_out, g_out)[0]
    if deep == 1:
        offsets = jnp.stack([xi, 1 - xi]) * (width // 2 // LANES)
        far = [[p, shift(p, "core")] for p in proj_far]
    else:
        proj_far = jnp.stack(proj_far)
        both = jnp.where(xi == 0, jnp.stack([proj_near, proj_far], 1), jnp.stack([proj_far, proj_near], 1))
        full = lax.all_gather(both, "dpo", axis=1, tiled=True)
        proj_near = full.reshape(2, width, -1)
        offsets = jnp.zeros((1,), jnp.int32)
        down = lax.all_gather(down, "dpo", axis=0, tiled=True)
        far = [None, None]
    other_near = shift(proj_near, "core")
    other_down = shift(down, "core")

    head = (width // LANES * 10 // 14) * LANES
    summed = [None] * nz
    grouped = [
        [grid_tokens[g][f][j] for j in range(ny) for f in range(2)] for g in range(nz)
    ]
    groups = list(range(1, nz)) + [0]
    near, down, *prepared, far_gate = prepare_group(
        offsets, info[groups[0]], grouped[groups[0]], [proj_near, other_near], [down, other_down], far[0], capacity
    )
    far_up = far[1]
    for i, g in enumerate(groups):
        far_head, near_heads, tails, far_up = expert_group(
            offsets, info[g], grouped[g], None if i else prepared, near, down, far_gate, far_up, i == 0, capacity, head
        )
        back = shift(far_head, "x")
        heads = [
            add(near_heads[j], back[j * tok_rows : (j + 1) * tok_rows]) for j in range(ny)
        ]
        summed[g] = (chain(heads, "y"), chain(tails, "y"))
    head_done = chain([s[0] for s in summed], "z")
    tail_done = chain([s[1] for s in summed], "z")
    tail_back = shift(tail_done[tok_rows:], "x")
    return jnp.concatenate([head_done, add(tail_done[:tok_rows], tail_back)], axis=1)


def solution(mesh):
    deep = mesh.shape["dp"] // PAIR
    chips = mesh.shape["expert"] // 2
    ny = 1
    while ny * ny * 4 <= chips:
        ny *= 2
    nz = chips // ny
    fine = Mesh(mesh.devices.reshape(deep, PAIR, nz, ny, 2), ("dpo", "x", "z", "y", "core"))
    dp, expert = ("dpo", "x"), ("z", "y", "core")
    everyone = dp + expert
    placed = (
        P(everyone, None),
        P(everyone, None),
        P(everyone, None),
        P(expert, None, dp, None),
        P(expert, None, dp, None),
        P(expert, None, dp, None),
        P(expert, None, dp, None),
        P(expert, dp, None),
        P(expert, dp, None),
        P(expert, dp, None),
        P(expert, dp, None),
    )
    return jax.shard_map(
        layer, mesh=fine, in_specs=placed, out_specs=P(everyone, None), check_vma=False
    )
```
